32 devices in a mesh: chan: 8 (over y, x, core), win: 4 (over z).
Axes of the slice: x: 2, y: 2, z: 4, core: 2. Of those that a mesh axis runs over, the one named last changes fastest.
Arguments:
- record: bfloat16 [128, 256, 2048], P('chan', 'win'), may hold values from -40 to 40
- owners: int32 [2], replicated, may hold values from 0 to 7, as said below
- pair_mask: int32 [2, 16, 128], P(None, None, 'chan'), may hold values 0 or 1
Outputs:
- cross: float32 [2, 16, 2, 128, 512], P(None, 'win', None, 'chan')
The draws below stay inside these ranges and needn't reach their ends.
Inputs may be any that keep to these rules, and one draw needn't show every extreme that they name: `owners`: the 2 planned blocks are all different, and the last block is always among them.
All inputs are finite; a program needn't handle non-finite values. No bound on the sum of `pair_mask` on one device may be relied on, other than what follows from the above.
Results may differ from the reference program's by a relative error of at most 0.0012.
Values may be sent and summed in bfloat16 or wider, within the bound.
No kernel may reach another device: no remote copies, remote signals or barrier semaphores. Data moves between devices by JAX's collectives and lax.ppermute only.
A program may use at most 128 MiB of HBM per device.

```python
import math
import jax
import jax.numpy as jnp
from jax import lax

CH_DEV = 16
SAMPLES = 2048
BINS = 512
STEPS = 2
CHANNELS = 128
WINDOWS = 256


def draw_record(key, part):
    keys = jax.random.split(key, 3)
    gains = jnp.exp(jax.random.uniform(keys[0], (CHANNELS, 1, 1), jnp.float32, math.log(0.3), math.log(3.0)))
    window_gains = jnp.exp(jax.random.uniform(keys[1], (1, WINDOWS, 1), jnp.float32, math.log(0.5), math.log(2.0)))
    noise = jnp.clip(jax.random.normal(keys[2], (CHANNELS, WINDOWS, SAMPLES), jnp.float32), -6.0, 6.0)
    return (gains * window_gains * noise).astype(jnp.bfloat16)


def draw_owners(key, part):
    block_count = CHANNELS // CH_DEV
    plan_key = jax.random.fold_in(key, 17)
    rotate_key = jax.random.fold_in(key, 29)
    others = jax.random.permutation(plan_key, block_count - 1)[:STEPS - 1].astype(jnp.int32)
    last_block = jnp.full((1,), block_count - 1, jnp.int32)
    plan = jnp.concatenate([others, last_block])
    offset = jax.random.randint(rotate_key, (), 0, STEPS)
    return jnp.roll(plan, offset).astype(jnp.int32)


def with_ends(result, stream_key, least, high):
    index_at = [jax.random.randint(jax.random.fold_in(stream_key, axis), (), 0, length) for axis, length in enumerate(result.shape)]
    widest = result.shape.index(max(result.shape))
    next_to = index_at[:widest] + [(index_at[widest] + 1) % result.shape[widest]] + index_at[widest + 1:]
    return result.at[tuple(index_at)].set(least).at[tuple(next_to)].set(high)


def setup_inputs(seed: int = 0) -> dict:
    key_of = jax.random.split(jax.random.key(seed), 4)
    record = draw_record(jax.random.fold_in(key_of[3], 71), 0)
    owners = draw_owners(jax.random.fold_in(key_of[3], 71), 0)
    pair_mask = with_ends((jax.random.randint(key_of[2], (STEPS, CH_DEV, CHANNELS), 0, 8) < 7).astype(jnp.int32), jax.random.fold_in(key_of[2], 1), 0, 1)
    return dict(record=record, owners=owners, pair_mask=pair_mask)


water_level = 0.25
epsilon = 1e-06

def fourier_table():
    sample_ids = jnp.arange(SAMPLES, dtype=jnp.int32)[:, None]
    bin_ids = jnp.arange(BINS, dtype=jnp.int32)[None, :]
    phases = 2.0 * math.pi / SAMPLES * (sample_ids * bin_ids % SAMPLES).astype(jnp.float32)
    return jnp.concatenate([jnp.cos(phases), -jnp.sin(phases)], axis=1).astype(jnp.bfloat16)

def whiten(channel_block, table):
    spectra = jnp.dot(channel_block.reshape(-1, SAMPLES), table, preferred_element_type=jnp.float32)
    spectra = spectra.reshape(channel_block.shape[0], channel_block.shape[1], 2, BINS)
    mean_power = lax.optimization_barrier(jnp.mean(spectra * spectra, axis=(2, 3), keepdims=True))
    magnitude = spectra[:, :, 0:1] * spectra[:, :, 0:1] + spectra[:, :, 1:2] * spectra[:, :, 1:2]
    return (spectra / jnp.sqrt(magnitude + water_level * mean_power + epsilon)).astype(jnp.bfloat16)

def correlate(source_rows, target_rows):
    src_real = source_rows[:, :, 0].astype(jnp.float32)
    src_imag = source_rows[:, :, 1].astype(jnp.float32)
    dst_real = target_rows[:, :, 0].astype(jnp.float32)
    dst_imag = target_rows[:, :, 1].astype(jnp.float32)
    real_part = jnp.einsum('iwk,jwk->ijk', src_real, dst_real) + jnp.einsum('iwk,jwk->ijk', src_imag, dst_imag)
    imag_part = jnp.einsum('iwk,jwk->ijk', src_real, dst_imag) - jnp.einsum('iwk,jwk->ijk', src_imag, dst_real)
    return jnp.stack([real_part, imag_part], axis=1)

def reference(record, owners, pair_mask):
    table = fourier_table()
    blocks = record.reshape(CHANNELS // CH_DEV, CH_DEV, WINDOWS, SAMPLES)

    def whiten_block(channel_block):
        return whiten(channel_block, table)
    whitened = lax.map(whiten_block, blocks)
    channel_ids = jnp.arange(CHANNELS, dtype=jnp.int32)
    results = []
    for step_index in range(STEPS):
        owner_block = owners[step_index]
        owned = whitened[owner_block]

        def against(target_block):
            return correlate(owned, target_block)
        stacked = lax.map(against, whitened)
        joined = jnp.transpose(stacked, (1, 2, 0, 3, 4)).reshape(CH_DEV, 2, CHANNELS, BINS)
        row_ids = owner_block * CH_DEV + jnp.arange(CH_DEV, dtype=jnp.int32)
        kept = ((channel_ids[None, :] >= row_ids[:, None]) & (pair_mask[step_index] == 1)).astype(jnp.float32)
        results.append(joined * (kept[:, None, :, None] / math.sqrt(WINDOWS)))
    return jnp.stack(results)
```

```python
import functools
import math

import jax
import jax.numpy as jnp
from jax import lax
from jax.experimental import pallas as pl
from jax.experimental.pallas import tpu as pltpu
from jax.sharding import PartitionSpec as P

BINS = 512
STEPS = 2
LANES = 128
FOLD = BINS // LANES

water_level = 0.25
epsilon = 1e-06


def twiddles(samples):
    digit = jnp.arange(24, dtype=jnp.int32)[:, None]
    factor = (digit % 8) * jnp.where(digit < 8, 1, jnp.where(digit < 16, 8, 64))
    sample_ids = jnp.arange(samples, dtype=jnp.int32)[None, :]
    phases = 2.0 * math.pi / samples * (sample_ids * factor % samples).astype(jnp.float32)
    return jnp.cos(phases), jnp.sin(phases)


def whiten_body(rec_ref, cos_ref, sin_ref, out_ref, rot_ref, table_ref, stage_ref):
    step = pl.program_id(0)
    block = rec_ref.shape[0]
    samples = rec_ref.shape[1]
    pairs = block // LANES

    @pl.when(step == 0)
    def _():
        def fill(k2, carry):
            for lane in range(0, samples, 512):
                cols = pl.ds(lane, 512)
                c0, s0 = cos_ref[0:8, cols], sin_ref[0:8, cols]
                c1, s1 = cos_ref[8:16, cols], sin_ref[8:16, cols]
                c2, s2 = cos_ref[pl.ds(16 + k2, 1), cols], sin_ref[pl.ds(16 + k2, 1), cols]
                cp, sp = c1 * c2 - s1 * s2, s1 * c2 + c1 * s2
                for k1 in range(0, 8, 2):
                    ca, sa = cp[k1 : k1 + 1], sp[k1 : k1 + 1]
                    cb, sb = cp[k1 + 1 : k1 + 2], sp[k1 + 1 : k1 + 2]
                    real = jnp.concatenate([ca * c0 - sa * s0, cb * c0 - sb * s0], axis=0)
                    imag = jnp.concatenate([sa * c0 + ca * s0, sb * c0 + cb * s0], axis=0)
                    row = pl.multiple_of(k2 * 64 + k1 * 8, 16)
                    table_ref[pl.ds(row, 16), cols] = real.astype(jnp.bfloat16)
                    table_ref[pl.ds(BINS + row, 16), cols] = (-imag).astype(jnp.bfloat16)
            return carry

        lax.fori_loop(0, 8, fill, 0)

    rec = rec_ref[...]
    contract = (((1,), (1,)), ((), ()))
    real = lax.dot_general(table_ref[0:BINS], rec, contract, preferred_element_type=jnp.float32)
    imag = lax.dot_general(
        table_ref[BINS : 2 * BINS], rec, contract, preferred_element_type=jnp.float32
    )
    power = real * real + imag * imag
    mean_power = jnp.sum(power, axis=0, keepdims=True) * (1.0 / (2 * BINS))
    scale = lax.rsqrt(power + (water_level * mean_power + epsilon))
    real, imag = real * scale, imag * scale
    low = lax.broadcasted_iota(jnp.int32, (BINS, LANES), 1) < LANES // 2
    for pair in range(pairs):
        r = real[:, pair * LANES : (pair + 1) * LANES]
        i = imag[:, pair * LANES : (pair + 1) * LANES]
        even = jnp.where(low, r, pltpu.roll(i, LANES // 2, 1))
        odd = jnp.where(low, pltpu.roll(r, LANES // 2, 1), i)
        for local, value in ((2 * pair, even), (2 * pair + 1, odd)):
            channel = step * (2 * pairs) + local
            for fold in range(FOLD):
                stage_ref[:, fold * 16 + channel, :] = value[fold * LANES : (fold + 1) * LANES]

    @pl.when(step == pl.num_programs(0) - 1)
    def _():
        rows = stage_ref.shape[1]
        low_half = lax.broadcasted_iota(jnp.int32, (rows, LANES), 1) < LANES // 2

        def emit(kt, carry):
            value = stage_ref[kt]
            out_ref[kt] = value.astype(jnp.bfloat16)
            turned = pltpu.roll(value, LANES // 2, 1)
            rot_ref[kt] = jnp.where(low_half, turned, -turned).astype(jnp.bfloat16)
            return carry

        lax.fori_loop(0, stage_ref.shape[0], emit, 0, unroll=4)


def whiten(record, cos_rows, sin_rows):
    channels, windows, samples = record.shape
    rows = channels * windows
    block = 256
    shape = jax.ShapeDtypeStruct((LANES, FOLD * channels, 2 * windows), jnp.bfloat16)
    whole = pl.BlockSpec(shape.shape, lambda s: (0, 0, 0))
    return pl.pallas_call(
        whiten_body,
        grid=(rows // block,),
        in_specs=[
            pl.BlockSpec((block, samples), lambda s: (s, 0)),
            pl.BlockSpec((24, samples), lambda s: (0, 0)),
            pl.BlockSpec((24, samples), lambda s: (0, 0)),
        ],
        out_specs=[whole, whole],
        out_shape=[shape, shape],
        scratch_shapes=[
            pltpu.VMEM((2 * BINS, samples), jnp.bfloat16),
            pltpu.VMEM(shape.shape, jnp.float32),
        ],
        compiler_params=pltpu.CompilerParams(vmem_limit_bytes=60 << 20),
        cost_estimate=pl.CostEstimate(
            flops=4 * rows * samples * BINS, bytes_accessed=8 << 20, transcendentals=0
        ),
        name="whiten",
    )(record.reshape(rows, samples), cos_rows, sin_rows)


def correlate_body(base_ref, src_ref, tgt_ref, rot_ref, out_ref, stage_ref):
    depth = src_ref.shape[0]
    chans = src_ref.shape[1] // FOLD
    lane_fold = lax.broadcasted_iota(jnp.int32, (chans, LANES), 1) // (2 * chans)
    for first in range(0, depth, 8):
        for kt in range(first, first + 8):
            pieces = []
            for fold in range(FOLD):
                rows = slice(fold * chans, (fold + 1) * chans)
                pieces += [tgt_ref[kt, rows], rot_ref[kt, rows]]
            weights = jnp.concatenate(pieces, axis=0)
            full = lax.dot_general(
                src_ref[kt],
                weights,
                (((1,), (1,)), ((), ())),
                preferred_element_type=jnp.float32,
            )
            kept = full[0:chans]
            for fold in range(1, FOLD):
                kept = jnp.where(
                    lane_fold == fold, full[fold * chans : (fold + 1) * chans], kept
                )
            stage_ref[kt - first] = kept
        for a in range(chans):
            out_ref[a, first : first + 8, :] = stage_ref[:, a, :]


def correlate(source, target, rotated, base):
    depth = 16
    steps = source.shape[0] // depth
    rows = source.shape[1]
    chans = rows // FOLD
    grid_spec = pltpu.PrefetchScalarGridSpec(
        num_scalar_prefetch=1,
        grid=(steps,),
        in_specs=[
            pl.BlockSpec((depth, rows, LANES), lambda s, b: (s, 0, 0)),
            pl.BlockSpec((depth, rows, LANES), lambda s, b: (b[0] // depth + s, 0, 0)),
            pl.BlockSpec((depth, rows, LANES), lambda s, b: (b[0] // depth + s, 0, 0)),
        ],
        out_specs=pl.BlockSpec((chans, depth, LANES), lambda s, b: (0, s, 0)),
        scratch_shapes=[pltpu.VMEM((8, chans, LANES), jnp.float32)],
    )
    return pl.pallas_call(
        correlate_body,
        grid_spec=grid_spec,
        out_shape=jax.ShapeDtypeStruct((chans, source.shape[0], LANES), jnp.float32),
        cost_estimate=pl.CostEstimate(
            flops=source.shape[0] * 2 * rows * LANES * LANES * 4,
            bytes_accessed=source.shape[0] * rows * LANES * 10,
            transcendentals=0,
        ),
        name="correlate",
    )(base.reshape(1), source, target, rotated)


def finish_body(count, sel_ref, keep_ref, *refs):
    own_parts, low_parts, high_parts = refs[:count], refs[count : 2 * count], refs[2 * count : 3 * count]
    out_ref, stage_ref = refs[3 * count :]
    last_step, core = sel_ref[0], sel_ref[1]
    rows = out_ref.shape[1]
    chans = out_ref.shape[3]
    half = LANES // 2

    def total(parts, a):
        value = parts[0][a]
        for part in parts[1:]:
            value = value + part[a]
        return value

    def emit(step, a, value):
        turned = value.T
        for fold in range(FOLD):
            for part in range(2):
                row = fold * 2 * chans + part * chans
                out_ref[step, a, part, :, fold * LANES : (fold + 1) * LANES] = (
                    turned[row : row + chans] * keep_ref[step, a]
                )

    for a in range(rows):
        emit(last_step, a, total(own_parts, a))
        stage_ref[pl.ds(pl.multiple_of(core * half, half), half), :] = total(low_parts, a)
        stage_ref[pl.ds(pl.multiple_of((1 - core) * half, half), half), :] = total(high_parts, a)
        emit(1 - last_step, a, stage_ref[...])


def finish(own_parts, low_parts, high_parts, keep, last_step, core):
    count = len(own_parts)
    rows = own_parts[0].shape[0]
    chans = keep.shape[2]
    vmem = pl.BlockSpec(memory_space=pltpu.VMEM)
    return pl.pallas_call(
        functools.partial(finish_body, count),
        in_specs=[pl.BlockSpec(memory_space=pltpu.SMEM)] + [vmem] * (3 * count + 1),
        out_specs=vmem,
        out_shape=jax.ShapeDtypeStruct((STEPS, rows, 2, chans, BINS), jnp.float32),
        scratch_shapes=[pltpu.VMEM((LANES, LANES), jnp.float32)],
        name="finish",
    )(jnp.stack([last_step, core]), keep, *own_parts, *low_parts, *high_parts)


def window_parts(partial, win_count):
    rows = partial.shape[0] // win_count
    here = lax.axis_index("win")
    parts = [lax.dynamic_slice_in_dim(partial, here * rows, rows, 0)]
    for hop in range(1, win_count):
        away = lax.dynamic_slice_in_dim(partial, (here ^ hop) * rows, rows, 0)
        parts.append(lax.ppermute(away, "win", [(i, i ^ hop) for i in range(win_count)]))
    return parts


def per_device(record, owners, pair_mask):
    channels, windows, samples = record.shape
    win_count = lax.axis_size("win")
    chan_count = lax.axis_size("chan")
    chan = lax.axis_index("chan")
    core = chan % 2
    last = chan_count - 1
    last_step = jnp.where(owners[0] == last, 0, 1).astype(jnp.int32)
    other = jnp.where(owners[0] == last, owners[1], owners[0])
    half = LANES // 2

    spectra, rotated = whiten(record, *twiddles(samples))

    swap = [(i, i ^ 1) for i in range(chan_count)]
    kept_half = lax.dynamic_slice_in_dim(spectra, core * half, half, 0)
    sent_half = lax.dynamic_slice_in_dim(spectra, (1 - core) * half, half, 0)
    current = jnp.where(other % 2 == core, kept_half, lax.ppermute(sent_half, "chan", swap))
    bits = list(range(1, chan_count.bit_length() - 1))
    for up, down in zip(bits, reversed(bits)):
        arrived = lax.ppermute(
            current,
            "chan",
            [(i, i ^ (1 << (down if i % 2 else up))) for i in range(chan_count)],
        )
        bit = jnp.where(core == 1, down, up)
        current = jnp.where(((other ^ chan) >> bit) & 1 == 1, arrived, current)
    partner = lax.ppermute(current, "chan", swap)

    own = correlate(spectra, spectra, rotated, jnp.zeros((), jnp.int32))
    own_parts = window_parts(own, win_count)
    low_parts = window_parts(correlate(current, spectra, rotated, core * half), win_count)
    high_parts = window_parts(correlate(partner, spectra, rotated, (1 - core) * half), win_count)

    rows = channels // win_count
    row_offset = lax.axis_index("win") * rows
    column_ids = chan * channels + jnp.arange(channels, dtype=jnp.int32)
    row_ids = owners[:, None] * channels + row_offset + jnp.arange(rows, dtype=jnp.int32)[None, :]
    quality = lax.dynamic_slice_in_dim(pair_mask, row_offset, rows, 1)
    kept = (column_ids[None, None, :] >= row_ids[:, :, None]) & (quality == 1)
    keep = kept.astype(jnp.float32) / math.sqrt(windows * win_count)
    keep = jnp.broadcast_to(keep[..., None], keep.shape + (LANES,))
    return finish(own_parts, low_parts, high_parts, keep, last_step, core)


def solution(mesh):
    placed = (P("chan", "win", None), P(), P(None, None, "chan"))
    return jax.shard_map(
        per_device,
        mesh=mesh,
        in_specs=placed,
        out_specs=P(None, "win", None, "chan", None),
        check_vma=False,
    )
```

```python
import functools
import math

import jax
import jax.numpy as jnp
from jax import lax
from jax.experimental import pallas as pl
from jax.experimental.pallas import tpu as pltpu
from jax.sharding import PartitionSpec as P


BINS = 512
STEPS = 2
LANES = 128
FOLD = BINS // LANES

water_level = 0.25
epsilon = 1e-06


def twiddles(samples):
    digit = jnp.arange(24, dtype=jnp.int32)[:, None]
    factor = (digit % 8) * jnp.where(digit < 8, 1, jnp.where(digit < 16, 8, 64))
    sample_ids = jnp.arange(samples, dtype=jnp.int32)[None, :]
    phases = 2.0 * math.pi / samples * (sample_ids * factor % samples).astype(jnp.float32)
    return jnp.cos(phases), jnp.sin(phases)


def whiten_body(rec_ref, cos_ref, sin_ref, out_ref, rot_ref, table_ref, stage_ref):
    step = pl.program_id(0)
    block = rec_ref.shape[0]
    samples = rec_ref.shape[1]
    pairs = block // LANES

    @pl.when(step == 0)
    def _():
        def fill(k2, carry):
            for lane in range(0, samples, 512):
                cols = pl.ds(lane, 512)
                c0, s0 = cos_ref[0:8, cols], sin_ref[0:8, cols]
                c1, s1 = cos_ref[8:16, cols], sin_ref[8:16, cols]
                c2, s2 = cos_ref[pl.ds(16 + k2, 1), cols], sin_ref[pl.ds(16 + k2, 1), cols]
                cp, sp = c1 * c2 - s1 * s2, s1 * c2 + c1 * s2
                for k1 in range(0, 8, 2):
                    ca, sa = cp[k1 : k1 + 1], sp[k1 : k1 + 1]
                    cb, sb = cp[k1 + 1 : k1 + 2], sp[k1 + 1 : k1 + 2]
                    real = jnp.concatenate([ca * c0 - sa * s0, cb * c0 - sb * s0], axis=0)
                    imag = jnp.concatenate([sa * c0 + ca * s0, sb * c0 + cb * s0], axis=0)
                    row = pl.multiple_of(k2 * 64 + k1 * 8, 16)
                    table_ref[pl.ds(row, 16), cols] = real.astype(jnp.bfloat16)
                    table_ref[pl.ds(BINS + row, 16), cols] = (-imag).astype(jnp.bfloat16)
            return carry

        lax.fori_loop(0, 8, fill, 0)

    rec = rec_ref[...]
    contract = (((1,), (1,)), ((), ()))
    real = lax.dot_general(table_ref[0:BINS], rec, contract, preferred_element_type=jnp.float32)
    imag = lax.dot_general(
        table_ref[BINS : 2 * BINS], rec, contract, preferred_element_type=jnp.float32
    )
    power = real * real + imag * imag
    mean_power = jnp.sum(power, axis=0, keepdims=True) * (1.0 / (2 * BINS))
    scale = lax.rsqrt(power + (water_level * mean_power + epsilon))
    real, imag = real * scale, imag * scale
    low = lax.broadcasted_iota(jnp.int32, (BINS, LANES), 1) < LANES // 2
    for pair in range(pairs):
        r = real[:, pair * LANES : (pair + 1) * LANES]
        i = imag[:, pair * LANES : (pair + 1) * LANES]
        even = jnp.where(low, r, pltpu.roll(i, LANES // 2, 1))
        odd = jnp.where(low, pltpu.roll(r, LANES // 2, 1), i)
        for local, value in ((2 * pair, even), (2 * pair + 1, odd)):
            channel = step * (2 * pairs) + local
            for fold in range(FOLD):
                stage_ref[:, fold * 16 + channel, :] = value[fold * LANES : (fold + 1) * LANES]

    @pl.when(step == pl.num_programs(0) - 1)
    def _():
        rows = out_ref.shape[1]
        low_half = lax.broadcasted_iota(jnp.int32, (rows, LANES), 1) < LANES // 2

        def emit(kt, carry):
            value = stage_ref[kt, 0:rows].astype(jnp.bfloat16)
            out_ref[kt] = value
            turned = pltpu.roll(value, LANES // 2, 1)
            rot_ref[kt] = jnp.where(low_half, turned, -turned)
            return carry

        lax.fori_loop(0, stage_ref.shape[0], emit, 0, unroll=16)


def whiten(record, cos_rows, sin_rows):
    channels, windows, samples = record.shape
    rows = channels * windows
    block = 256
    shape = jax.ShapeDtypeStruct((LANES, FOLD * channels, 2 * windows), jnp.bfloat16)
    whole = pl.BlockSpec(shape.shape, lambda s: (0, 0, 0))
    return pl.pallas_call(
        whiten_body,
        grid=(rows // block,),
        in_specs=[
            pl.BlockSpec((block, samples), lambda s: (s, 0)),
            pl.BlockSpec((24, samples), lambda s: (0, 0)),
            pl.BlockSpec((24, samples), lambda s: (0, 0)),
        ],
        out_specs=[whole, whole],
        out_shape=[shape, shape],
        scratch_shapes=[
            pltpu.VMEM((2 * BINS, samples), jnp.bfloat16),
            pltpu.VMEM((LANES, FOLD * channels + 8, LANES), jnp.float32),
        ],
        compiler_params=pltpu.CompilerParams(vmem_limit_bytes=60 << 20),
        cost_estimate=pl.CostEstimate(
            flops=4 * rows * samples * BINS, bytes_accessed=8 << 20, transcendentals=0
        ),
        name="whiten",
    )(record.reshape(rows, samples), cos_rows, sin_rows)


def correlate_block(src_ref, tgt_ref, rot_ref, out_ref, stage_ref):
    depth = src_ref.shape[0]
    chans = src_ref.shape[1] // FOLD
    lane_fold = lax.broadcasted_iota(jnp.int32, (chans, LANES), 1) // (2 * chans)
    for first in range(0, depth, 8):
        for kt in range(first, first + 8):
            pieces = []
            for fold in range(FOLD):
                rows = slice(fold * chans, (fold + 1) * chans)
                pieces += [tgt_ref[kt, rows], rot_ref[kt, rows]]
            weights = jnp.concatenate(pieces, axis=0)
            full = lax.dot_general(
                src_ref[kt],
                weights,
                (((1,), (1,)), ((), ())),
                preferred_element_type=jnp.float32,
            )
            kept = full[0:chans]
            for fold in range(1, FOLD):
                kept = jnp.where(
                    lane_fold == fold, full[fold * chans : (fold + 1) * chans], kept
                )
            stage_ref[kt - first] = kept
        for a in range(chans):
            out_ref[a, first : first + 8, :] = stage_ref[:, a, :]


def correlate_body(steps, base_ref, *refs):
    sources, rest = refs[:-4], refs[-4:]
    if len(sources) == 1:
        correlate_block(sources[0], *rest)
        return
    for index, source in enumerate(sources):

        @pl.when(pl.program_id(0) // steps == index)
        def _():
            correlate_block(source, *rest)


def correlate(sources, target, rotated, bases):
    depth = 16
    count = len(sources)
    length, rows, _ = sources[0].shape
    steps = length // depth
    chans = rows // FOLD

    def source_map(n):
        return lambda s, b: (jnp.clip(s - n * steps, 0, steps - 1), 0, 0)

    def target_map(s, b):
        return (b[s // steps] // depth + s % steps, 0, 0)

    block = (depth, rows, LANES)
    grid_spec = pltpu.PrefetchScalarGridSpec(
        num_scalar_prefetch=1,
        grid=(count * steps,),
        in_specs=[pl.BlockSpec(block, source_map(n)) for n in range(count)]
        + [pl.BlockSpec(block, target_map)] * 2,
        out_specs=pl.BlockSpec((chans, depth, LANES), lambda s, b: (0, s, 0)),
        scratch_shapes=[pltpu.VMEM((8, chans, LANES), jnp.float32)],
    )
    return pl.pallas_call(
        functools.partial(correlate_body, steps),
        grid_spec=grid_spec,
        out_shape=jax.ShapeDtypeStruct((chans, count * length, LANES), jnp.float32),
        cost_estimate=pl.CostEstimate(
            flops=count * length * 2 * rows * LANES * LANES * 4,
            bytes_accessed=count * length * rows * LANES * 10,
            transcendentals=0,
        ),
        name="correlate",
    )(bases, *sources, target, rotated)


def finish_body(sel_ref, keep_ref, own_ref, *refs):
    chunk_refs, (out_ref, stage_ref) = refs[:-2], refs[-2:]
    last_step, core = sel_ref[0], sel_ref[1]
    rows = out_ref.shape[1]
    chans = out_ref.shape[3]
    half = LANES // 2
    piece = half // len(chunk_refs)

    def emit(step, a, value):
        turned = value.T
        for fold in range(FOLD):
            for part in range(2):
                row = fold * 2 * chans + part * chans
                out_ref[step, a, part, :, fold * LANES : (fold + 1) * LANES] = (
                    turned[row : row + chans] * keep_ref[step, a]
                )

    for a in range(rows):
        emit(last_step, a, own_ref[a])
        for index, chunk_ref in enumerate(chunk_refs):
            for side, start in enumerate((core * half, (1 - core) * half)):
                row = pl.multiple_of(start + index * piece, piece)
                stage_ref[pl.ds(row, piece), :] = chunk_ref[a, side * piece : (side + 1) * piece]
        emit(1 - last_step, a, stage_ref[...])


def finish(own, chunks, keep, last_step, core):
    rows = own.shape[0]
    chans = keep.shape[2]
    vmem = pl.BlockSpec(memory_space=pltpu.VMEM)
    return pl.pallas_call(
        finish_body,
        in_specs=[pl.BlockSpec(memory_space=pltpu.SMEM)] + [vmem] * (2 + len(chunks)),
        out_specs=vmem,
        out_shape=jax.ShapeDtypeStruct((STEPS, rows, 2, chans, BINS), jnp.float32),
        scratch_shapes=[pltpu.VMEM((LANES, LANES), jnp.float32)],
        name="finish",
    )(jnp.stack([last_step, core]), keep, own, *chunks)


def window_sum(partial, win_count, wire, only=None):
    rows = partial.shape[0] // win_count
    here = lax.axis_index("win")
    arrived = []
    for hop in range(1, win_count):
        away = lax.dynamic_slice_in_dim(partial, (here ^ hop) * rows, rows, 0).astype(wire)
        pairs = [(i, i ^ hop) for i in range(win_count)]
        if only is None:
            arrived.append(lax.ppermute(away, "win", pairs))
        else:
            base = only * win_count
            arrived.append(
                lax.ppermute(away, ("chan", "win"), [(base + i, base + j) for i, j in pairs])
            )
    total = lax.dynamic_slice_in_dim(partial, here * rows, rows, 0)
    for part in arrived:
        total = total + part.astype(jnp.float32)
    return total


CHUNKS = 2
WIRE = jnp.float16


def planned(record, owners, pair_mask):
    channels, windows, samples = record.shape
    win_count = lax.axis_size("win")
    chan_count = lax.axis_size("chan")
    chan = lax.axis_index("chan")
    core = chan % 2
    last = chan_count - 1
    last_step = jnp.where(owners[0] == last, 0, 1).astype(jnp.int32)
    other = jnp.where(owners[0] == last, owners[1], owners[0])
    half = LANES // 2
    piece = half // CHUNKS

    spectra, rotated = whiten(record, *twiddles(samples))

    swap = [(i, i ^ 1) for i in range(chan_count)]
    bits = list(range(1, chan_count.bit_length() - 1))
    currents = []
    for index in range(CHUNKS):
        sent = lax.dynamic_slice_in_dim(spectra, (1 - core) * half + index * piece, piece, 0)
        arrived = lax.ppermute(sent, "chan", swap)
        kept = lax.dynamic_slice_in_dim(spectra, core * half + index * piece, piece, 0)
        currents.append(jnp.where(other % 2 == core, kept, arrived))
    for up, down in zip(bits, reversed(bits)):
        pairs = [(i, i ^ (1 << (down if i % 2 else up))) for i in range(chan_count)]
        bit = jnp.where(core == 1, down, up)
        for index in range(CHUNKS):
            arrived = lax.ppermute(currents[index], "chan", pairs)
            currents[index] = jnp.where(((other ^ chan) >> bit) & 1 == 1, arrived, currents[index])

    own = correlate([spectra], spectra, rotated, jnp.zeros((1,), jnp.int32))
    own = window_sum(own, win_count, jnp.float32, only=last)
    chunks = []
    for index in range(CHUNKS):
        partner = lax.ppermute(currents[index], "chan", swap)
        bases = jnp.stack([core * half, (1 - core) * half]) + index * piece
        partial = correlate([currents[index], partner], spectra, rotated, bases)
        chunks.append(window_sum(partial, win_count, WIRE))

    rows = channels // win_count
    row_offset = lax.axis_index("win") * rows
    column_ids = chan * channels + jnp.arange(channels, dtype=jnp.int32)
    row_ids = owners[:, None] * channels + row_offset + jnp.arange(rows, dtype=jnp.int32)[None, :]
    quality = lax.dynamic_slice_in_dim(pair_mask, row_offset, rows, 1)
    kept = (column_ids[None, None, :] >= row_ids[:, :, None]) & (quality == 1)
    keep = kept.astype(jnp.float32) / math.sqrt(windows * win_count)
    keep = jnp.broadcast_to(keep[..., None], keep.shape + (LANES,))
    return finish(own, chunks, keep, last_step, core)


def solution(mesh):
    placed = (P("chan", "win", None), P(), P(None, None, "chan"))
    return jax.shard_map(
        planned,
        mesh=mesh,
        in_specs=placed,
        out_specs=P(None, "win", None, "chan", None),
        check_vma=False,
    )
```
